32 devices in a mesh: row: 4 (over x, core), col: 8 (over z, y).
Axes of the slice: x: 2, y: 2, z: 4, core: 2. Of those that a mesh axis runs over, the one named last changes fastest.
Arguments:
- matrix: float32 [24576, 24576], P('row', 'col'), may hold values from -6 to 6
Outputs:
- y_block: float32 [4, 24576], P(None, 'row')
- reflectors: float32 [4, 24576], P(None, 'row')
- t_factor: float32 [4, 4], replicated
The draws below stay inside these ranges and needn't reach their ends.
All inputs are finite; a program needn't handle non-finite values.
Results may differ from the reference program's by a relative error of at most 0.0003.
Values sent between devices are 32-bit elements; how exact they have to be, the bound alone decides.
A program may use at most 128 MiB of HBM per device.

```python
import jax
import jax.numpy as jnp
from jax import lax

N = 24576
K = 4


def steps_of(rng, shape, split, smallest, top_value):
    level = 1.0
    for dim, shards_of in split:
        heights = jax.random.uniform(jax.random.fold_in(jax.random.fold_in(rng, 6), dim), (shards_of,), jnp.float32, smallest / len(split), top_value / len(split))
        level = level * jnp.repeat(jnp.exp(heights), shape[dim] // shards_of).reshape((-1,) + (1,) * (len(shape) - 1 - dim))
    return level


def normal_values(key, shape, scale, bound, shards=(), held_as=jnp.bfloat16):
    gain = steps_of(key, shape, shards, -0.22, 0.18) if shards else 1.0
    values = jax.random.normal(key, shape, jnp.float32) * scale * gain
    return jnp.minimum(jnp.maximum(values, -bound), bound).astype(held_as)


def setup_inputs(seed: int = 0) -> dict:
    key_list = jax.random.split(jax.random.key(seed), 2)
    matrix = normal_values(key_list[0], (N, N), 1.0, 6.0, ((0, 4), (1, 8)), jnp.float32)
    return dict(matrix=matrix)


precise = lax.Precision.HIGHEST

def householder(pivot_value, squares):
    length = jnp.sqrt(pivot_value * pivot_value + squares)
    signed = jnp.where(pivot_value >= 0, 1.0, -1.0)
    diagonal = -signed * length
    factor = (diagonal - pivot_value) / diagonal
    return (factor, pivot_value - diagonal)

def finish(product, cross_dots, y_rows, t_block, factor, panel_step):
    new_column = factor * (product - jnp.dot(cross_dots, y_rows, precision=precise))
    t_column = -factor * jnp.dot(t_block, cross_dots, precision=precise)
    slots = jnp.arange(K, dtype=jnp.int32)
    t_column = jnp.where(slots == panel_step, factor, t_column)
    t_block = jnp.where(slots[None, :] == panel_step, t_column[:, None], t_block)
    y_rows = jnp.where(slots[:, None] == panel_step, new_column[None, :], y_rows)
    return (y_rows, t_block)

def reference(matrix):
    extent = matrix.shape[0]
    all_rows = jnp.arange(extent, dtype=jnp.int32)
    slots = jnp.arange(K, dtype=jnp.int32)

    def advance(panel_step, carried):
        y_rows, v_rows, t_block = carried
        column = lax.dynamic_index_in_dim(matrix, panel_step, 1, keepdims=False)
        v_entry = lax.dynamic_index_in_dim(v_rows, panel_step, 1, keepdims=False)
        column = column - jnp.dot(v_entry, y_rows, precision=precise)
        left_dots = jnp.dot(v_rows, column, precision=precise)
        column = column - jnp.dot(jnp.dot(t_block.T, left_dots, precision=precise), v_rows, precision=precise)
        below = all_rows > panel_step + 1
        squares = jnp.sum(jnp.where(below, column * column, 0.0))
        pivot_value = lax.dynamic_index_in_dim(column, panel_step + 1, 0, keepdims=False)
        factor, divisor = householder(pivot_value, squares)
        reflect = jnp.where(below, column / divisor, 0.0) + (all_rows == panel_step + 1).astype(column.dtype)
        product = jnp.dot(matrix, reflect, precision=precise)
        cross_dots = jnp.dot(v_rows, reflect, precision=precise)
        y_rows, t_block = finish(product, cross_dots, y_rows, t_block, factor, panel_step)
        v_rows = jnp.where(slots[:, None] == panel_step, reflect[None, :], v_rows)
        return (y_rows, v_rows, t_block)
    start = (jnp.zeros((K, extent), jnp.float32), jnp.zeros((K, extent), jnp.float32), jnp.zeros((K, K), jnp.float32))
    y_rows, v_rows, t_block = lax.fori_loop(0, K, advance, start)
    return (y_rows, v_rows, t_block)
```

```python
import functools

import jax
import jax.numpy as jnp
from jax import lax
from jax.experimental import pallas as pl
from jax.experimental.pallas import tpu as pltpu
from jax.sharding import PartitionSpec as P

K = 4
LANES = 128
MESH = pl.DeviceIdType.MESH
VMEM_BYTES = 67043328
SPARE_BYTES = 5 * 2**19


def plan(R, C, rows, cols):
    q = C // R
    m = cols // LANES
    G = 8 if m % 8 == 0 else m
    ng = m // G
    groups = q * ng
    room = (VMEM_BYTES - SPARE_BYTES) // (LANES * cols * 4)
    slots = min(groups * G, room) // 2 * 2
    assert 2 * slots >= groups * G and slots >= q and G % 2 == 0 and slots % 2 == 0
    return q, m, G, ng, groups, slots


def lane_total(row):
    return jnp.sum(row, axis=-1, keepdims=True)


def kernel(
    R, C, a_hbm, o_ref, t_ref,
    pool, acc, pan, av, xs, pbuf, rbuf, lbuf, sbuf, rnd, vy, ob, oav, ox, vs, ys, ps, kept, index,
    pool_sem, pan_sem, pan_send, av_sem, p_send, p_recv, s_send, s_recv, o_send, o_recv,
):
    rows, cols = a_hbm.shape
    q, m, G, ng, groups, slots = plan(R, C, rows, cols)
    tiles = groups * G
    spill = tiles - slots
    r = lax.axis_index("row")
    c = lax.axis_index("col")

    def send(src, dst, send_sem, recv_sem, tr, tc):
        same = jnp.logical_and(tr == r, tc == c)

        @pl.when(jnp.logical_not(same))
        def _():
            pltpu.make_async_remote_copy(
                src, dst, send_sem, recv_sem, device_id=(tr, tc), device_id_type=MESH
            ).start()

        @pl.when(same)
        def _():
            pltpu.make_async_copy(src, dst, recv_sem).start()

    def sent(src, dst, send_sem, recv_sem, tr, tc):
        same = jnp.logical_and(tr == r, tc == c)

        @pl.when(jnp.logical_not(same))
        def _():
            pltpu.make_async_remote_copy(
                src, dst, send_sem, recv_sem, device_id=(tr, tc), device_id_type=MESH
            ).wait_send()

    def arrived(ref, sem):
        pltpu.make_async_copy(ref, ref, sem).wait()

    def panel_copy(t):
        return pltpu.make_async_copy(
            a_hbm.at[pl.ds(pl.multiple_of(t * LANES, LANES), LANES), pl.ds(0, LANES)],
            pool.at[
                slots - q + lax.div(t, m), :,
                pl.ds(pl.multiple_of(lax.rem(t, m) * LANES, LANES), LANES),
            ],
            pan_sem,
        )

    @pl.when(c == 0)
    def _():
        @pl.loop(0, q * m)
        def _(t):
            panel_copy(t).start()

    def tile_copy(t):
        slot = lax.rem(t, slots)
        row = pl.multiple_of(t * LANES, LANES)
        return pltpu.make_async_copy(
            a_hbm.at[pl.ds(row, LANES)], pool.at[slot], pool_sem.at[slot]
        )

    @pl.loop(0, slots - q)
    def _(t):
        tile_copy(t).start()

    barrier = pltpu.get_barrier_semaphore()
    me = r * C + c

    @pl.loop(1, R * C)
    def _(k):
        t = lax.rem(me + k, R * C)
        pl.semaphore_signal(
            barrier, inc=1, device_id=(lax.div(t, C), lax.rem(t, C)), device_id_type=MESH
        )

    def panel_sends(act):
        for part in range(2):
            for piece in range(q):
                for tr in range(R):
                    first, count = (0, 1) if part == 0 else (1, K)
                    act(
                        pan.at[pl.ds(first, count), pl.ds(piece * ng, ng)],
                        av.at[pl.ds(first, count)],
                        pan_send.at[part, piece, tr],
                        av_sem.at[part],
                        jnp.int32(tr),
                        r * q + piece,
                    )

    @pl.when(c == 0)
    def _():
        arrived(pool.at[pl.ds(slots - q, q)], pan_sem)

        @pl.loop(0, groups)
        def _(g):
            slot = slots - q + lax.div(g, ng)
            for s in range(G):
                at = pl.multiple_of((lax.rem(g, ng) * G + s) * LANES, LANES)
                turned = pool[slot, :, pl.ds(at, LANES)].T
                for k in range(K + 1):
                    pan[k, g, s : s + 1, :] = turned[k : k + 1, :]

    @pl.loop(slots - q, slots)
    def _(t):
        tile_copy(t).start()

    pl.semaphore_wait(barrier, R * C - 1)

    @pl.when(c == 0)
    def _():
        panel_sends(send)

    sub = lax.broadcasted_iota(jnp.int32, (G, LANES), 0)
    lane = lax.broadcasted_iota(jnp.int32, (G, LANES), 1)
    for n in range(ng):
        index[n] = c * cols + (n * G + sub) * LANES + lane
    for g in range(groups):
        index[ng + g] = r * rows + (g * G + sub) * LANES + lane
    lane1 = lax.broadcasted_iota(jnp.int32, (1, LANES), 1)
    first_col = (jnp.zeros((1, LANES), jnp.int32) + c) == 0

    def load(ref, *at):
        return [ref[(*at, n)] for n in range(ng)]

    def store(ref, value, *at):
        for n in range(ng):
            ref[(*at, n)] = value[n]

    def pick(row, k):
        return lane_total(jnp.where(lane1 == k, row, 0.0))

    def dots(one, two):
        total = one[0] * two[0]
        for n in range(1, ng):
            total = total + one[n] * two[n]
        return jnp.sum(total, axis=0, keepdims=True)

    def less(value, scale, other):
        return [a - scale * b for a, b in zip(value, other)]

    def round_copy(j, k, o):
        tc = lax.rem(c + o, C)
        return pltpu.make_async_remote_copy(
            sbuf.at[j, k], rnd.at[j, k, c], s_send.at[j, k], s_recv.at[j, k],
            device_id=(r, tc), device_id_type=MESH,
        )

    def round_send(j, k):
        rnd[j, k, c] = sbuf[j, k]

        @pl.loop(1, C)
        def _(o):
            round_copy(j, k, o).start()

    def round_get(j, k):
        arrived(rnd.at[j, k, pl.ds(0, C - 1)], s_recv.at[j, k])
        total = rnd[j, k, 0]
        for n in range(1, C):
            total = total + rnd[j, k, n]
        return total

    def places():
        return [index[n] for n in range(ng)]

    def keep(at, value):
        kept[at : at + 1, :] = jnp.broadcast_to(value, (1, LANES))

    def row_of(at):
        return kept[at : at + 1, :]

    def scalar(at):
        return kept[at : at + 1, 0:1]

    def T_AT(i, j):
        return i * K + j

    def CROSS_AT(i, j):
        return K * K + i * K + j

    def TOP_AT(i):
        return 2 * K * K + i

    def p_targets(j, g):
        if j + 1 == K:
            for tc in range(C):
                send(
                    pbuf.at[j, g], lbuf.at[c, g], p_send.at[j], p_recv.at[j], r, jnp.int32(tc)
                )
            return
        piece, part = lax.div(g, ng), lax.rem(g, ng)
        for tr in range(R):
            send(
                pbuf.at[j, g], rbuf.at[j, c, part], p_send.at[j], p_recv.at[j],
                jnp.int32(tr), r * q + piece,
            )

    def p_sent(j):
        if j + 1 == K:
            arrived(lbuf.at[pl.ds(0, C - 1)], p_send.at[j])
            return
        own = lax.div(c, q) == r

        @pl.when(own)
        def _():
            arrived(rbuf.at[j, pl.ds(0, C - 1)], p_send.at[j])

        @pl.when(jnp.logical_not(own))
        def _():
            arrived(rbuf.at[j], p_send.at[j])

    def o_targets(src, dst, k):
        for u in range(q):
            send(
                src, dst.at[lax.rem(c, q)], o_send.at[k], o_recv.at[k], lax.div(c, q), r + R * u
            )

    def o_sent(dst, k):
        own = jnp.logical_and(lax.div(c, q) == r, lax.rem(c, R) == r)

        @pl.when(own)
        def _():
            arrived(dst.at[pl.ds(0, q - 1)], o_send.at[k])

        @pl.when(jnp.logical_not(own))
        def _():
            arrived(dst, o_send.at[k])

    def r_sent(j, k):
        arrived(rnd.at[j, k, pl.ds(0, C - 1)], s_send.at[j, k])

    def line(j, tile, slot):
        pbuf[j, lax.div(tile, G), pl.ds(lax.rem(tile, G), 1), :] = jnp.sum(
            acc[slot].T, axis=0, keepdims=True
        )

    def multiply(j):
        back = j % 2 == 1
        xb = [
            jnp.broadcast_to(xs[t // G, t % G : t % G + 1, :], (8, LANES)) for t in range(m)
        ]

        def tile_at(at):
            return tiles - 1 - at if back else at

        def finish(at):
            for w in range(2):
                line(j, tile_at(at + w), lax.rem(lax.div(at, 2), 2) * 2 + w)

        @pl.loop(0, tiles // 2)
        def _(pair):
            at = pair * 2
            @pl.loop(jnp.maximum(at, slots) if j else at, at + 2)
            def _(k):
                tile_copy(tile_at(k)).wait()

            finish(jnp.maximum(at - 2, 0))
            for w in range(2):
                slot = lax.rem(tile_at(at + w), slots)
                for u in range(0, LANES, 8):
                    total = None
                    for t in range(m):
                        term = pool[slot, u : u + 8, t * LANES : (t + 1) * LANES] * xb[t]
                        total = term if total is None else total + term
                    acc[lax.rem(pair, 2) * 2 + w, u : u + 8, :] = total

            @pl.loop(at, jnp.minimum(at + 2, spill))
            def _(k):
                tile_copy(tile_at(slots + k)).start()

            full = jnp.logical_and(at > 0, lax.rem(at, G) == 0)

            @pl.loop(0, full.astype(jnp.int32))
            def _(k):
                p_targets(j, lax.div(tile_at(at - 1), G))

        finish(jnp.int32(tiles - 2))
        p_targets(j, jnp.int32(0 if back else groups - 1))

    for w in range(2):
        acc[w] = jnp.zeros((LANES, LANES), jnp.float32)
    zero = jnp.zeros((1, 1), jnp.float32)
    arrived(av.at[pl.ds(0, 1)], av_sem.at[0])

    for j in range(K):
        if j == 0:
            x = load(av, 0)
        store(xs, [jnp.where(w > j + 1, a, 0.0) for w, a in zip(places(), x)])
        x_top_row = jnp.where(first_col, x[0][0:1, :], 0.0)
        sbuf[j, 0] = jnp.zeros((8, LANES), jnp.float32)
        sbuf[j, 1] = jnp.zeros((8, LANES), jnp.float32)
        sbuf[j, 0 if j else 1, K + 1 : K + 2, :] = x_top_row

        if j:
            for i in range(j):
                sbuf[j, 0, i : i + 1, :] = dots(load(vs, i), x)
            round_send(j, 0)
            o_targets(vy.at[j - 1], ob.at[j - 1], j - 1)
            if j == 1:
                o_targets(av, oav, K)
            if j + 1 == K:
                o_targets(xs, ox, j)
        else:
            b = load(xs)
            sbuf[j, 1, K : K + 1, :] = dots(b, b)
            round_send(j, 1)
        multiply(j)

        if j:
            got = round_get(j, 0)
            left = [lane_total(got[i : i + 1, :]) for i in range(j)]
            w = []
            for k in range(j):
                total = zero
                for i in range(k + 1):
                    total = total + scalar(T_AT(i, k)) * left[i]
                w.append(total)
            b, b_top = load(xs), got[K + 1 : K + 2, :]
            for i in range(j):
                b = less(b, w[i], load(vs, i))
                b_top = b_top - w[i] * row_of(TOP_AT(i))
            b = [jnp.where(at > j + 1, a, 0.0) for at, a in zip(places(), b)]
            for i in range(j):
                sbuf[j, 1, i : i + 1, :] = dots(load(vs, i), b)
            sbuf[j, 1, K : K + 1, :] = dots(b, b)
            round_send(j, 1)
            p_sent(j - 1)
            r_sent(j - 1, 1)
            if j > 1:
                o_sent(ob.at[j - 2], j - 2)
                r_sent(j - 1, 0)
        else:
            w = []

            @pl.when(c == 0)
            def _():
                panel_sends(sent)

        got = round_get(j, 1)
        if j == 0:
            b_top = got[K + 1 : K + 2, :]
            arrived(av.at[pl.ds(1, K)], av_sem.at[1])
        v_top = [row_of(TOP_AT(i)) for i in range(j)]
        squares = lane_total(got[K : K + 1, :])
        pivot = pick(b_top, j + 1)
        length = jnp.sqrt(pivot * pivot + squares)
        beta = -jnp.where(pivot >= 0, 1.0, -1.0) * length
        tau = (beta - pivot) / beta
        div = pivot - beta
        cross = [lane_total(got[i : i + 1, :]) / div + pick(v_top[i], j + 1) for i in range(j)]
        new_top = jnp.where(lane1 > j + 1, b_top / div, 0.0) + jnp.where(lane1 == j + 1, 1.0, 0.0)
        keep(TOP_AT(j), new_top)
        for i in range(j):
            total = zero
            for k in range(i, j):
                total = total + scalar(T_AT(i, k)) * cross[k]
            keep(T_AT(i, j), -tau * total)
            keep(CROSS_AT(i, j), cross[i])
        keep(T_AT(j, j), tau)
        back = []
        for k in range(j + 2 if j else 0):
            total = zero
            for i in range(j):
                total = total + w[i] * pick(v_top[i], k)
            back.append(total)

        if j + 1 == K:
            break

        v = [a / div + jnp.where(at == j + 1, 1.0, 0.0) for at, a in zip(places(), b)]
        store(vs, v, j)
        store(vy, v, j, 1)
        fix = [jnp.zeros((G, LANES), jnp.float32)] * ng
        for i in range(j):
            fix = less(fix, w[i], load(ps, i))
        for k, value in enumerate(back):
            fix = less(fix, -value, load(av, k))
        y_fix = load(av, j + 1)
        for i in range(j):
            y_fix = less(y_fix, cross[i], load(ys, i))
        x = load(av, j + 1)
        for i in range(j):
            x = less(x, pick(v_top[i], j + 1), load(ys, i))
        entry = pick(new_top, j + 1)

        arrived(rbuf.at[j], p_recv.at[j])
        p = load(rbuf, j, 0)
        for n in range(1, C):
            p = [a + b_ for a, b_ in zip(p, load(rbuf, j, n))]
        p = [(a + e) / div for a, e in zip(p, fix)]
        y = [tau * (a + e) for a, e in zip(p, y_fix)]
        x = less(x, entry, y)
        store(vy, y, j, 0)
        store(ys, y, j)
        store(ps, [a + e for a, e in zip(p, load(av, j + 1))], j)

    scale = tau / div
    y_part, a_part = [], []
    for i in range(K - 1):
        total = w[i] / scalar(T_AT(i, i))
        for k in range(i + 1, K - 1):
            total = total + w[k] * scalar(CROSS_AT(i, k))
        y_part.append(-tau * (total / div + cross[i]))
    for k in range(K + 1):
        a_part.append(scale * back[k] + (tau if k == K else 0.0))
    for j in range(K - 1):
        arrived(ob.at[j], o_recv.at[j])
    arrived(ox, o_recv.at[K - 1])
    arrived(oav, o_recv.at[K])
    for g in range(groups):
        h, n = g // ng, g % ng
        at = index[ng + g]
        b = ox[h, n]
        rest = a_part[0] * oav[h, 0, n]
        for k in range(1, K + 1):
            rest = rest + a_part[k] * oav[h, k, n]
        for i in range(K - 1):
            y, v = ob[i, h, 0, n], ob[i, h, 1, n]
            o_ref[i, h, 0, n] = y
            o_ref[i, h, 1, n] = v
            b = b - w[i] * v
            rest = rest + y_part[i] * y
        v = jnp.where(at > K, b, 0.0) / div + jnp.where(at == K, 1.0, 0.0)
        o_ref[K - 1, h, 1, n] = v
        o_ref[K - 1, h, 0, n] = rest

    ti = lax.broadcasted_iota(jnp.int32, (K, K), 0)
    tj = lax.broadcasted_iota(jnp.int32, (K, K), 1)
    t_all = jnp.zeros((K, K), jnp.float32)
    for j in range(K):
        for i in range(j + 1):
            t_all = jnp.where(jnp.logical_and(ti == i, tj == j), scalar(T_AT(i, j)), t_all)
    t_ref[...] = t_all

    r_sent(K - 1, 0)
    r_sent(K - 1, 1)
    o_sent(ob.at[K - 2], K - 2)
    o_sent(ox, K - 1)
    o_sent(oav, K)
    arrived(lbuf, p_recv.at[K - 1])
    for g in range(groups):
        total = lbuf[0, g]
        for n in range(1, C):
            total = total + lbuf[n, g]
        h, n = g // ng, g % ng
        o_ref[K - 1, h, 0, n] = scale * total + o_ref[K - 1, h, 0, n]
    p_sent(K - 1)


def lay_out(o_ref, t_in, y_ref, v_ref, t_ref):
    _, q, _, ng, G, _ = o_ref.shape
    for h in range(q):
        for n in range(ng):
            for s in range(G):
                at = ((h * ng + n) * G + s) * LANES
                for j in range(K):
                    y_ref[j : j + 1, at : at + LANES] = o_ref[j, h, 0, n, s : s + 1, :]
                    v_ref[j : j + 1, at : at + LANES] = o_ref[j, h, 1, n, s : s + 1, :]
    t_ref[...] = t_in[...]


def solution(mesh):
    R, C = mesh.shape["row"], mesh.shape["col"]

    def on_device(matrix):
        rows, cols = matrix.shape
        q, m, G, ng, groups, slots = plan(R, C, rows, cols)
        f32 = lambda *shape: pltpu.VMEM(shape, jnp.float32)
        dma = lambda *shape: pltpu.SemaphoreType.DMA(shape)
        blocks, t_block = pl.pallas_call(
            functools.partial(kernel, R, C),
            out_shape=(
                jax.ShapeDtypeStruct((K, q, 2, ng, G, LANES), jnp.float32),
                jax.ShapeDtypeStruct((K, K), jnp.float32),
            ),
            in_specs=[pl.BlockSpec(memory_space=pl.ANY)],
            out_specs=(pl.BlockSpec(memory_space=pltpu.VMEM),) * 2,
            scratch_shapes=[
                f32(slots, LANES, cols),
                f32(4, LANES, LANES),
                f32(K + 1, groups, G, LANES),
                f32(K + 1, ng, G, LANES),
                f32(ng, G, LANES),
                f32(K, groups, G, LANES),
                f32(K - 1, C, ng, G, LANES),
                f32(C, groups, G, LANES),
                f32(K, 2, 8, LANES),
                f32(K, 2, C, 8, LANES),
                f32(K - 1, 2, ng, G, LANES),
                f32(K - 1, q, 2, ng, G, LANES),
                f32(q, K + 1, ng, G, LANES),
                f32(q, ng, G, LANES),
                f32(K - 1, ng, G, LANES),
                f32(K - 1, ng, G, LANES),
                f32(K - 1, ng, G, LANES),
                f32(2 * K * K + K, LANES),
                pltpu.VMEM((ng + groups, G, LANES), jnp.int32),
                dma(slots),
                pltpu.SemaphoreType.DMA,
                dma(2, q, R),
                dma(2),
                dma(K),
                dma(K),
                dma(K, 2),
                dma(K, 2),
                dma(K + 1),
                dma(K + 1),
            ],
            compiler_params=pltpu.CompilerParams(
                collective_id=0, has_side_effects=True, vmem_limit_bytes=VMEM_BYTES,

            ),
        )(matrix)
        return pl.pallas_call(
            lay_out,
            out_shape=(
                jax.ShapeDtypeStruct((K, rows), jnp.float32),
                jax.ShapeDtypeStruct((K, rows), jnp.float32),
                jax.ShapeDtypeStruct((K, K), jnp.float32),
            ),
            in_specs=[pl.BlockSpec(memory_space=pltpu.VMEM)] * 2,
            out_specs=(pl.BlockSpec(memory_space=pltpu.VMEM),) * 3,
        )(blocks, t_block)

    return jax.shard_map(
        on_device,
        mesh=mesh,
        in_specs=(P("row", "col"),),
        out_specs=(P(None, "row"), P(None, "row"), P()),
        check_vma=False,
    )
```

```python
import functools

import jax
import jax.numpy as jnp
from jax import lax
from jax.experimental import pallas as pl
from jax.experimental.pallas import tpu as pltpu
from jax.sharding import PartitionSpec as P

K = 4
LANES = 128
MESH = pl.DeviceIdType.MESH
VMEM_BYTES = 67043328
SPARE_BYTES = 5 * 2**19


def plan(R, C, rows, cols):
    q = C // R
    m = cols // LANES
    G = 8 if m % 8 == 0 else m
    ng = m // G
    groups = q * ng
    room = (VMEM_BYTES - SPARE_BYTES) // (LANES * cols * 4)
    slots = min(groups * G, room) // 2 * 2
    assert 2 * slots >= groups * G and slots >= q and G % 2 == 0 and slots % 2 == 0
    return q, m, G, ng, groups, slots


def lane_total(row):
    return jnp.sum(row, axis=-1, keepdims=True)


def kernel(
    R, C, a_hbm, o_ref, t_ref,
    pool, acc, pan, av, xs, pbuf, rbuf, lbuf, sbuf, rnd, vy, ob, oav, ox, vs, ys, ps, bs, kept, index,
    pool_sem, pan_sem, pan_send, av_sem, p_send, p_recv, s_send, s_recv, o_send, o_recv,
):
    rows, cols = a_hbm.shape
    q, m, G, ng, groups, slots = plan(R, C, rows, cols)
    tiles = groups * G
    spill = tiles - slots
    r = lax.axis_index("row")
    c = lax.axis_index("col")

    def send(src, dst, send_sem, recv_sem, tr, tc):
        same = jnp.logical_and(tr == r, tc == c)

        @pl.when(jnp.logical_not(same))
        def _():
            pltpu.make_async_remote_copy(
                src, dst, send_sem, recv_sem, device_id=(tr, tc), device_id_type=MESH
            ).start()

        @pl.when(same)
        def _():
            pltpu.make_async_copy(src, dst, recv_sem).start()

    def sent(src, dst, send_sem, recv_sem, tr, tc):
        same = jnp.logical_and(tr == r, tc == c)

        @pl.when(jnp.logical_not(same))
        def _():
            pltpu.make_async_remote_copy(
                src, dst, send_sem, recv_sem, device_id=(tr, tc), device_id_type=MESH
            ).wait_send()

    def arrived(ref, sem):
        pltpu.make_async_copy(ref, ref, sem).wait()

    def panel_copy(t):
        return pltpu.make_async_copy(
            a_hbm.at[pl.ds(pl.multiple_of(t * LANES, LANES), LANES), pl.ds(0, LANES)],
            pool.at[
                slots - q + lax.div(t, m), :,
                pl.ds(pl.multiple_of(lax.rem(t, m) * LANES, LANES), LANES),
            ],
            pan_sem,
        )

    @pl.when(c == 0)
    def _():
        @pl.loop(0, q * m)
        def _(t):
            panel_copy(t).start()

    def tile_copy(t):
        slot = lax.rem(t, slots)
        row = pl.multiple_of(t * LANES, LANES)
        return pltpu.make_async_copy(
            a_hbm.at[pl.ds(row, LANES)], pool.at[slot], pool_sem.at[slot]
        )

    @pl.loop(0, slots - q)
    def _(t):
        tile_copy(t).start()

    barrier = pltpu.get_barrier_semaphore()
    me = r * C + c

    @pl.loop(1, R * C)
    def _(k):
        t = lax.rem(me + k, R * C)
        pl.semaphore_signal(
            barrier, inc=1, device_id=(lax.div(t, C), lax.rem(t, C)), device_id_type=MESH
        )

    def panel_sends(act):
        for part in range(2):
            for piece in range(q):
                for tr in range(R):
                    first, count = (0, 1) if part == 0 else (1, K)
                    act(
                        pan.at[pl.ds(first, count), pl.ds(piece * ng, ng)],
                        av.at[pl.ds(first, count)],
                        pan_send.at[part, piece, tr],
                        av_sem.at[part],
                        jnp.int32(tr),
                        r * q + piece,
                    )

    @pl.when(c == 0)
    def _():
        arrived(pool.at[pl.ds(slots - q, q)], pan_sem)

        @pl.loop(0, groups)
        def _(g):
            slot = slots - q + lax.div(g, ng)
            for s in range(G):
                at = pl.multiple_of((lax.rem(g, ng) * G + s) * LANES, LANES)
                turned = pool[slot, :, pl.ds(at, LANES)].T
                for k in range(K + 1):
                    pan[k, g, s : s + 1, :] = turned[k : k + 1, :]

    @pl.loop(slots - q, slots)
    def _(t):
        tile_copy(t).start()

    pl.semaphore_wait(barrier, R * C - 1)

    @pl.when(c == 0)
    def _():
        panel_sends(send)

    sub = lax.broadcasted_iota(jnp.int32, (G, LANES), 0)
    lane = lax.broadcasted_iota(jnp.int32, (G, LANES), 1)
    for n in range(ng):
        index[n] = c * cols + (n * G + sub) * LANES + lane
    for g in range(groups):
        index[ng + g] = r * rows + (g * G + sub) * LANES + lane
    lane1 = lax.broadcasted_iota(jnp.int32, (1, LANES), 1)
    first_col = (jnp.zeros((1, LANES), jnp.int32) + c) == 0

    def load(ref, *at):
        return [ref[(*at, n)] for n in range(ng)]

    def store(ref, value, *at):
        for n in range(ng):
            ref[(*at, n)] = value[n]

    def pick(row, k):
        return lane_total(jnp.where(lane1 == k, row, 0.0))

    def dots(one, two):
        total = one[0] * two[0]
        for n in range(1, ng):
            total = total + one[n] * two[n]
        return jnp.sum(total, axis=0, keepdims=True)

    def less(value, scale, other):
        return [a - scale * b for a, b in zip(value, other)]

    def round_copy(j, k, o):
        tc = lax.rem(c + o, C)
        return pltpu.make_async_remote_copy(
            sbuf.at[j, k], rnd.at[j, k, c], s_send.at[j, k], s_recv.at[j, k],
            device_id=(r, tc), device_id_type=MESH,
        )

    def round_send(j, k):
        rnd[j, k, c] = sbuf[j, k]

        @pl.loop(1, C)
        def _(o):
            round_copy(j, k, o).start()

    def round_get(j, k):
        arrived(rnd.at[j, k, pl.ds(0, C - 1)], s_recv.at[j, k])
        total = rnd[j, k, 0]
        for n in range(1, C):
            total = total + rnd[j, k, n]
        return total

    def places():
        return [index[n] for n in range(ng)]

    def keep(at, value):
        kept[at : at + 1, :] = jnp.broadcast_to(value, (1, LANES))

    def row_of(at):
        return kept[at : at + 1, :]

    def scalar(at):
        return kept[at : at + 1, 0:1]

    def T_AT(i, j):
        return i * K + j

    def CROSS_AT(i, j):
        return K * K + i * K + j

    def TOP_AT(i):
        return 2 * K * K + i

    def push(src, dst, send_sem, recv_sem, tr, tc):
        pltpu.make_async_remote_copy(
            src, dst, send_sem, recv_sem, device_id=(tr, tc), device_id_type=MESH
        ).start()

    def W_AT(i):
        return 2 * K * K + K + i

    def p_targets(j, g, count=1):
        block = pbuf.at[j, pl.ds(g, count)]
        if j + 1 == K:
            for o in range(1, C):
                push(
                    block, lbuf.at[c, pl.ds(g, count)], p_send.at[j], p_recv.at[j], r,
                    lax.rem(c + o, C),
                )
            for n in range(count):
                lbuf[c, g + n] = pbuf[j, g + n]
            return
        piece, part = lax.div(g, ng), lax.rem(g, ng)
        there, tc = rbuf.at[j, c, pl.ds(part, count)], r * q + piece
        for o in range(1, R):
            push(block, there, p_send.at[j], p_recv.at[j], lax.rem(r + o, R), tc)
        send(block, there, p_send.at[j], p_recv.at[j], r, tc)

    def p_sent(j):
        if j + 1 == K:
            arrived(lbuf.at[pl.ds(0, C - 1)], p_send.at[j])
            return
        own = lax.div(c, q) == r

        @pl.when(own)
        def _():
            arrived(rbuf.at[j, pl.ds(0, C - 1)], p_send.at[j])

        @pl.when(jnp.logical_not(own))
        def _():
            arrived(rbuf.at[j], p_send.at[j])

    def o_targets(src, dst, k):
        for u in range(q):
            send(
                src, dst.at[lax.rem(c, q)], o_send.at[k], o_recv.at[k], lax.div(c, q), r + R * u
            )

    def o_sent(dst, k):
        own = jnp.logical_and(lax.div(c, q) == r, lax.rem(c, R) == r)

        @pl.when(own)
        def _():
            arrived(dst.at[pl.ds(0, q - 1)], o_send.at[k])

        @pl.when(jnp.logical_not(own))
        def _():
            arrived(dst, o_send.at[k])

    def r_sent(j, k):
        arrived(rnd.at[j, k, pl.ds(0, C - 1)], s_send.at[j, k])

    def line(j, tile, slot):
        pbuf[j, lax.div(tile, G), pl.ds(lax.rem(tile, G), 1), :] = jnp.sum(
            acc[slot].T, axis=0, keepdims=True
        )

    def multiply(j, late):
        back = j % 2 == 1

        def tile_at(at):
            return tiles - 1 - at if back else at

        def finish(at):
            for w in range(2):
                line(j, tile_at(at + w), lax.rem(lax.div(at, 2), 2) * 2 + w)

        def pairs(low, count, done):
            xb = [
                jnp.broadcast_to(xs[t // G, t % G : t % G + 1, :], (8, LANES))
                for t in range(m)
            ]

            @pl.loop(0, count // 2)
            def _(pair):
                at = low + pair * 2
                if j == 0:
                    for w in range(2):
                        tile_copy(tile_at(at + w)).wait()
                half = lax.rem(lax.div(at, 2), 2) * 2
                for w in range(2):
                    line(j, tile_at(jnp.maximum(at - 2, done) + w), 2 - half + w)
                for w in range(2):
                    slot = lax.rem(tile_at(at + w), slots)
                    for u in range(0, LANES, 8):
                        total = None
                        for t in range(m):
                            term = pool[slot, u : u + 8, t * LANES : (t + 1) * LANES] * xb[t]
                            total = term if total is None else total + term
                        acc[half + w, u : u + 8, :] = total

        if j == 0:
            @pl.loop(0, groups)
            def _(k):
                start = k * G
                pairs(start, G, start)
                finish(start + G - 2)
                p_targets(j, lax.div(tile_at(start), G))

                @pl.loop(start, jnp.minimum(start + G, spill))
                def _(at):
                    tile_copy(tile_at(slots + at)).start()
            return

        ends = [k * ng for k in range(1, q + 1)]
        if ng > 1:
            ends.append(groups - 1)
        cuts = sorted({0, *ends, min(groups, pl.cdiv(spill, G)), slots // G})
        sent_to = 0
        for low, high in zip(cuts, cuts[1:]):
            if low == cuts[-2]:
                late()

            if high * G > slots:
                @pl.loop(max(low * G, slots), high * G)
                def _(at):
                    tile_copy(tile_at(at)).wait()

            pairs(low * G, (high - low) * G, sent_to * G)
            if high in ends:
                finish(jnp.int32(high * G - 2))
                first = groups - high if back else sent_to
                p_targets(j, jnp.int32(first), high - sent_to)
                sent_to = high
            if low * G < spill:
                @pl.loop(low * G, min(high * G, spill))
                def _(at):
                    tile_copy(tile_at(slots + at)).start()

    for w in range(4):
        acc[w] = jnp.zeros((LANES, LANES), jnp.float32)
    zero = jnp.zeros((1, 1), jnp.float32)
    arrived(av.at[pl.ds(0, 1)], av_sem.at[0])

    for j in range(K):
        if j == 0:
            x = load(av, 0)
        store(xs, [jnp.where(w > j + 1, a, 0.0) for w, a in zip(places(), x)])
        x_top_row = jnp.where(first_col, x[0][0:1, :], 0.0)
        sbuf[j, 0] = jnp.zeros((8, LANES), jnp.float32)
        sbuf[j, 1] = jnp.zeros((8, LANES), jnp.float32)
        sbuf[j, 0 if j else 1, K + 1 : K + 2, :] = x_top_row

        if j:
            for i in range(j):
                sbuf[j, 0, i : i + 1, :] = dots(load(vs, i), x)
            round_send(j, 0)
            if j + 1 == K:
                o_targets(vy.at[j - 1], ob.at[j - 1], j - 1)
            if j == 1:
                o_targets(av, oav, K)
            if j + 1 == K:
                o_targets(xs, ox, j)
        else:
            b = load(xs)
            sbuf[j, 1, K : K + 1, :] = dots(b, b)
            round_send(j, 1)
        def second_round():
            got = round_get(j, 0)
            left = [lane_total(got[i : i + 1, :]) for i in range(j)]
            b, b_top = load(xs), got[K + 1 : K + 2, :]
            for k in range(j):
                total = zero
                for i in range(k + 1):
                    total = total + scalar(T_AT(i, k)) * left[i]
                keep(W_AT(k), total)
                b = less(b, total, load(vs, k))
                b_top = b_top - total * row_of(TOP_AT(k))
            keep(W_AT(K), b_top)
            b = [jnp.where(at > j + 1, a, 0.0) for at, a in zip(places(), b)]
            store(bs, b)
            for i in range(j):
                sbuf[j, 1, i : i + 1, :] = dots(load(vs, i), b)
            sbuf[j, 1, K : K + 1, :] = dots(b, b)
            round_send(j, 1)

        multiply(j, second_round)

        if j:
            w = [scalar(W_AT(i)) for i in range(j)]
            b, b_top = load(bs), row_of(W_AT(K))
            if j + 1 < K:
                o_targets(vy.at[j - 1], ob.at[j - 1], j - 1)
            p_sent(j - 1)
            r_sent(j - 1, 1)
            if j > 1:
                o_sent(ob.at[j - 2], j - 2)
                r_sent(j - 1, 0)
        else:
            w = []

            @pl.when(c == 0)
            def _():
                panel_sends(sent)

        got = round_get(j, 1)
        if j == 0:
            b_top = got[K + 1 : K + 2, :]
            arrived(av.at[pl.ds(1, K)], av_sem.at[1])
        v_top = [row_of(TOP_AT(i)) for i in range(j)]
        squares = lane_total(got[K : K + 1, :])
        pivot = pick(b_top, j + 1)
        length = jnp.sqrt(pivot * pivot + squares)
        beta = -jnp.where(pivot >= 0, 1.0, -1.0) * length
        tau = (beta - pivot) / beta
        div = pivot - beta
        cross = [lane_total(got[i : i + 1, :]) / div + pick(v_top[i], j + 1) for i in range(j)]
        new_top = jnp.where(lane1 > j + 1, b_top / div, 0.0) + jnp.where(lane1 == j + 1, 1.0, 0.0)
        keep(TOP_AT(j), new_top)
        for i in range(j):
            total = zero
            for k in range(i, j):
                total = total + scalar(T_AT(i, k)) * cross[k]
            keep(T_AT(i, j), -tau * total)
            keep(CROSS_AT(i, j), cross[i])
        keep(T_AT(j, j), tau)
        back = []
        for k in range(j + 2 if j else 0):
            total = zero
            for i in range(j):
                total = total + w[i] * pick(v_top[i], k)
            back.append(total)

        if j + 1 == K:
            break

        v = [a / div + jnp.where(at == j + 1, 1.0, 0.0) for at, a in zip(places(), b)]
        store(vs, v, j)
        store(vy, v, j, 1)
        fix = [jnp.zeros((G, LANES), jnp.float32)] * ng
        for i in range(j):
            fix = less(fix, w[i], load(ps, i))
        for k, value in enumerate(back):
            fix = less(fix, -value, load(av, k))
        y_fix = load(av, j + 1)
        for i in range(j):
            y_fix = less(y_fix, cross[i], load(ys, i))
        x = load(av, j + 1)
        for i in range(j):
            x = less(x, pick(v_top[i], j + 1), load(ys, i))
        entry = pick(new_top, j + 1)

        arrived(rbuf.at[j], p_recv.at[j])
        p = load(rbuf, j, 0)
        for n in range(1, C):
            p = [a + b_ for a, b_ in zip(p, load(rbuf, j, n))]
        p = [(a + e) / div for a, e in zip(p, fix)]
        y = [tau * (a + e) for a, e in zip(p, y_fix)]
        x = less(x, entry, y)
        store(vy, y, j, 0)
        store(ys, y, j)
        store(ps, [a + e for a, e in zip(p, load(av, j + 1))], j)

    scale = tau / div
    y_part, a_part = [], []
    for i in range(K - 1):
        total = w[i] / scalar(T_AT(i, i))
        for k in range(i + 1, K - 1):
            total = total + w[k] * scalar(CROSS_AT(i, k))
        y_part.append(-tau * (total / div + cross[i]))
    for k in range(K + 1):
        a_part.append(scale * back[k] + (tau if k == K else 0.0))
    for j in range(K - 1):
        arrived(ob.at[j], o_recv.at[j])
    arrived(ox, o_recv.at[K - 1])
    arrived(oav, o_recv.at[K])
    for g in range(groups):
        h, n = g // ng, g % ng
        at = index[ng + g]
        b = ox[h, n]
        rest = a_part[0] * oav[h, 0, n]
        for k in range(1, K + 1):
            rest = rest + a_part[k] * oav[h, k, n]
        for i in range(K - 1):
            y, v = ob[i, h, 0, n], ob[i, h, 1, n]
            o_ref[i, h, 0, n] = y
            o_ref[i, h, 1, n] = v
            b = b - w[i] * v
            rest = rest + y_part[i] * y
        v = jnp.where(at > K, b, 0.0) / div + jnp.where(at == K, 1.0, 0.0)
        o_ref[K - 1, h, 1, n] = v
        o_ref[K - 1, h, 0, n] = rest

    ti = lax.broadcasted_iota(jnp.int32, (K, K), 0)
    tj = lax.broadcasted_iota(jnp.int32, (K, K), 1)
    t_all = jnp.zeros((K, K), jnp.float32)
    for j in range(K):
        for i in range(j + 1):
            t_all = jnp.where(jnp.logical_and(ti == i, tj == j), scalar(T_AT(i, j)), t_all)
    t_ref[...] = t_all

    r_sent(K - 1, 0)
    r_sent(K - 1, 1)
    o_sent(ob.at[K - 2], K - 2)
    o_sent(ox, K - 1)
    o_sent(oav, K)
    arrived(lbuf.at[pl.ds(0, C - 1)], p_recv.at[K - 1])
    for g in range(groups):
        total = lbuf[0, g]
        for n in range(1, C):
            total = total + lbuf[n, g]
        h, n = g // ng, g % ng
        o_ref[K - 1, h, 0, n] = scale * total + o_ref[K - 1, h, 0, n]
    p_sent(K - 1)


def lay_out(o_ref, t_in, y_ref, v_ref, t_ref):
    _, q, _, ng, G, _ = o_ref.shape
    for h in range(q):
        for n in range(ng):
            for s in range(G):
                at = ((h * ng + n) * G + s) * LANES
                for j in range(K):
                    y_ref[j : j + 1, at : at + LANES] = o_ref[j, h, 0, n, s : s + 1, :]
                    v_ref[j : j + 1, at : at + LANES] = o_ref[j, h, 1, n, s : s + 1, :]
    t_ref[...] = t_in[...]


def solution(mesh):
    R, C = mesh.shape["row"], mesh.shape["col"]

    def on_device(matrix):
        rows, cols = matrix.shape
        q, m, G, ng, groups, slots = plan(R, C, rows, cols)
        f32 = lambda *shape: pltpu.VMEM(shape, jnp.float32)
        dma = lambda *shape: pltpu.SemaphoreType.DMA(shape)
        blocks, t_block = pl.pallas_call(
            functools.partial(kernel, R, C),
            out_shape=(
                jax.ShapeDtypeStruct((K, q, 2, ng, G, LANES), jnp.float32),
                jax.ShapeDtypeStruct((K, K), jnp.float32),
            ),
            in_specs=[pl.BlockSpec(memory_space=pl.ANY)],
            out_specs=(pl.BlockSpec(memory_space=pltpu.VMEM),) * 2,
            scratch_shapes=[
                f32(slots, LANES, cols),
                f32(4, LANES, LANES),
                f32(K + 1, groups, G, LANES),
                f32(K + 1, ng, G, LANES),
                f32(ng, G, LANES),
                f32(K, groups, G, LANES),
                f32(K - 1, C, ng, G, LANES),
                f32(C, groups, G, LANES),
                f32(K, 2, 8, LANES),
                f32(K, 2, C, 8, LANES),
                f32(K - 1, 2, ng, G, LANES),
                f32(K - 1, q, 2, ng, G, LANES),
                f32(q, K + 1, ng, G, LANES),
                f32(q, ng, G, LANES),
                f32(K - 1, ng, G, LANES),
                f32(K - 1, ng, G, LANES),
                f32(K - 1, ng, G, LANES),
                f32(ng, G, LANES),
                f32(2 * K * K + 2 * K + 1, LANES),
                pltpu.VMEM((ng + groups, G, LANES), jnp.int32),
                dma(slots),
                pltpu.SemaphoreType.DMA,
                dma(2, q, R),
                dma(2),
                dma(K),
                dma(K),
                dma(K, 2),
                dma(K, 2),
                dma(K + 1),
                dma(K + 1),
            ],
            compiler_params=pltpu.CompilerParams(
                collective_id=0, has_side_effects=True, vmem_limit_bytes=VMEM_BYTES,

            ),
        )(matrix)
        return pl.pallas_call(
            lay_out,
            out_shape=(
                jax.ShapeDtypeStruct((K, rows), jnp.float32),
                jax.ShapeDtypeStruct((K, rows), jnp.float32),
                jax.ShapeDtypeStruct((K, K), jnp.float32),
            ),
            in_specs=[pl.BlockSpec(memory_space=pltpu.VMEM)] * 2,
            out_specs=(pl.BlockSpec(memory_space=pltpu.VMEM),) * 3,
        )(blocks, t_block)

    return jax.shard_map(
        on_device,
        mesh=mesh,
        in_specs=(P("row", "col"),),
        out_specs=(P(None, "row"), P(None, "row"), P()),
        check_vma=False,
    )
```

```python
import functools

import jax
import jax.numpy as jnp
from jax import lax
from jax.experimental import pallas as pl
from jax.experimental.pallas import tpu as pltpu
from jax.sharding import PartitionSpec as P

K = 4
LANES = 128
MESH = pl.DeviceIdType.MESH
VMEM_BYTES = 67043328
SPARE_BYTES = 5 * 2**19


def plan(R, C, rows, cols):
    q = C // R
    m = cols // LANES
    G = 8 if m % 8 == 0 else m
    ng = m // G
    groups = q * ng
    room = (VMEM_BYTES - SPARE_BYTES) // (LANES * cols * 4)
    slots = min(groups * G, room) // 2 * 2
    assert 2 * slots >= groups * G and slots >= q and G % 2 == 0 and slots % 2 == 0
    return q, m, G, ng, groups, slots


def lane_total(row):
    return jnp.sum(row, axis=-1, keepdims=True)


def kernel(
    R, C, a_hbm, o_ref, t_ref,
    pool, acc, pan, av, xs, pbuf, rbuf, lbuf, sbuf, rnd, vy, ob, oav, ox, vs, ys, ps, bs, kept, index,
    pool_sem, pan_sem, pan_send, av_sem, p_send, p_recv, s_send, s_recv, o_send, o_recv,
):
    rows, cols = a_hbm.shape
    q, m, G, ng, groups, slots = plan(R, C, rows, cols)
    tiles = groups * G
    spill = tiles - slots
    r = lax.axis_index("row")
    c = lax.axis_index("col")

    def send(src, dst, send_sem, recv_sem, tr, tc):
        same = jnp.logical_and(tr == r, tc == c)

        @pl.when(jnp.logical_not(same))
        def _():
            pltpu.make_async_remote_copy(
                src, dst, send_sem, recv_sem, device_id=(tr, tc), device_id_type=MESH
            ).start()

        @pl.when(same)
        def _():
            pltpu.make_async_copy(src, dst, recv_sem).start()

    def sent(src, dst, send_sem, recv_sem, tr, tc):
        same = jnp.logical_and(tr == r, tc == c)

        @pl.when(jnp.logical_not(same))
        def _():
            pltpu.make_async_remote_copy(
                src, dst, send_sem, recv_sem, device_id=(tr, tc), device_id_type=MESH
            ).wait_send()

    def arrived(ref, sem):
        pltpu.make_async_copy(ref, ref, sem).wait()

    def panel_copy(t):
        return pltpu.make_async_copy(
            a_hbm.at[pl.ds(pl.multiple_of(t * LANES, LANES), LANES), pl.ds(0, LANES)],
            pool.at[
                slots - q + lax.div(t, m), :,
                pl.ds(pl.multiple_of(lax.rem(t, m) * LANES, LANES), LANES),
            ],
            pan_sem,
        )

    @pl.when(c == 0)
    def _():
        @pl.loop(0, q * m)
        def _(t):
            panel_copy(t).start()

    def tile_copy(t):
        slot = lax.rem(t, slots)
        row = pl.multiple_of(t * LANES, LANES)
        return pltpu.make_async_copy(
            a_hbm.at[pl.ds(row, LANES)], pool.at[slot], pool_sem.at[slot]
        )

    @pl.loop(0, slots - q)
    def _(t):
        tile_copy(t).start()

    barrier = pltpu.get_barrier_semaphore()
    me = r * C + c

    @pl.loop(1, R * C)
    def _(k):
        t = lax.rem(me + k, R * C)
        pl.semaphore_signal(
            barrier, inc=1, device_id=(lax.div(t, C), lax.rem(t, C)), device_id_type=MESH
        )

    def panel_sends(act):
        for part in range(2):
            for piece in range(q):
                for tr in range(R):
                    first, count = (0, 1) if part == 0 else (1, K)
                    act(
                        pan.at[pl.ds(first, count), pl.ds(piece * ng, ng)],
                        av.at[pl.ds(first, count)],
                        pan_send.at[part, piece, tr],
                        av_sem.at[part],
                        jnp.int32(tr),
                        r * q + piece,
                    )

    @pl.when(c == 0)
    def _():
        arrived(pool.at[pl.ds(slots - q, q)], pan_sem)

        @pl.loop(0, groups)
        def _(g):
            slot = slots - q + lax.div(g, ng)
            for s in range(G):
                at = pl.multiple_of((lax.rem(g, ng) * G + s) * LANES, LANES)
                turned = pool[slot, :, pl.ds(at, LANES)].T
                for k in range(K + 1):
                    pan[k, g, s : s + 1, :] = turned[k : k + 1, :]

    @pl.loop(slots - q, slots)
    def _(t):
        tile_copy(t).start()

    pl.semaphore_wait(barrier, R * C - 1)

    @pl.when(c == 0)
    def _():
        panel_sends(send)

    sub = lax.broadcasted_iota(jnp.int32, (G, LANES), 0)
    lane = lax.broadcasted_iota(jnp.int32, (G, LANES), 1)
    for n in range(ng):
        index[n] = c * cols + (n * G + sub) * LANES + lane
    for g in range(groups):
        index[ng + g] = r * rows + (g * G + sub) * LANES + lane
    lane1 = lax.broadcasted_iota(jnp.int32, (1, LANES), 1)
    first_col = (jnp.zeros((1, LANES), jnp.int32) + c) == 0

    def load(ref, *at):
        return [ref[(*at, n)] for n in range(ng)]

    def store(ref, value, *at):
        for n in range(ng):
            ref[(*at, n)] = value[n]

    def pick(row, k):
        return lane_total(jnp.where(lane1 == k, row, 0.0))

    def dots(one, two):
        total = one[0] * two[0]
        for n in range(1, ng):
            total = total + one[n] * two[n]
        return jnp.sum(total, axis=0, keepdims=True)

    def less(value, scale, other):
        return [a - scale * b for a, b in zip(value, other)]

    def round_copy(j, k, o):
        tc = lax.rem(c + o, C)
        return pltpu.make_async_remote_copy(
            sbuf.at[j, k], rnd.at[j, k, c], s_send.at[j, k], s_recv.at[j, k],
            device_id=(r, tc), device_id_type=MESH,
        )

    def round_send(j, k):
        rnd[j, k, c] = sbuf[j, k]

        @pl.loop(1, C)
        def _(o):
            round_copy(j, k, o).start()

    def round_get(j, k):
        arrived(rnd.at[j, k, pl.ds(0, C - 1)], s_recv.at[j, k])
        total = rnd[j, k, 0]
        for n in range(1, C):
            total = total + rnd[j, k, n]
        return total

    def places():
        return [index[n] for n in range(ng)]

    def keep(at, value):
        kept[at : at + 1, :] = jnp.broadcast_to(value, (1, LANES))

    def row_of(at):
        return kept[at : at + 1, :]

    def scalar(at):
        return kept[at : at + 1, 0:1]

    def T_AT(i, j):
        return i * K + j

    def CROSS_AT(i, j):
        return K * K + i * K + j

    def TOP_AT(i):
        return 2 * K * K + i

    def push(src, dst, send_sem, recv_sem, tr, tc):
        pltpu.make_async_remote_copy(
            src, dst, send_sem, recv_sem, device_id=(tr, tc), device_id_type=MESH
        ).start()

    def W_AT(i):
        return 2 * K * K + K + i

    def p_targets(j, g, count=1):
        block = pbuf.at[j, pl.ds(g, count)]
        if j + 1 == K:
            for o in range(1, C):
                push(
                    block, lbuf.at[c, pl.ds(g, count)], p_send.at[j], p_recv.at[j], r,
                    lax.rem(c + o, C),
                )
            for n in range(count):
                lbuf[c, g + n] = pbuf[j, g + n]
            return
        piece, part = lax.div(g, ng), lax.rem(g, ng)
        there, tc = rbuf.at[j, c, pl.ds(part, count)], r * q + piece
        for o in range(1, R):
            push(block, there, p_send.at[j], p_recv.at[j], lax.rem(r + o, R), tc)
        send(block, there, p_send.at[j], p_recv.at[j], r, tc)

    def p_sent(j):
        if j + 1 == K:
            arrived(lbuf.at[pl.ds(0, C - 1)], p_send.at[j])
            return
        own = lax.div(c, q) == r

        @pl.when(own)
        def _():
            arrived(rbuf.at[j, pl.ds(0, C - 1)], p_send.at[j])

        @pl.when(jnp.logical_not(own))
        def _():
            arrived(rbuf.at[j], p_send.at[j])

    def o_targets(src, dst, k):
        for u in range(q):
            send(
                src, dst.at[lax.rem(c, q)], o_send.at[k], o_recv.at[k], lax.div(c, q), r + R * u
            )

    def o_sent(dst, k):
        own = jnp.logical_and(lax.div(c, q) == r, lax.rem(c, R) == r)

        @pl.when(own)
        def _():
            arrived(dst.at[pl.ds(0, q - 1)], o_send.at[k])

        @pl.when(jnp.logical_not(own))
        def _():
            arrived(dst, o_send.at[k])

    def r_sent(j, k):
        arrived(rnd.at[j, k, pl.ds(0, C - 1)], s_send.at[j, k])

    def line(j, tile, slot):
        pbuf[j, lax.div(tile, G), pl.ds(lax.rem(tile, G), 1), :] = jnp.sum(
            acc[slot].T, axis=0, keepdims=True
        )

    def multiply(j, late):
        back = j % 2 == 1

        def tile_at(at):
            return tiles - 1 - at if back else at

        def finish(at):
            for w in range(2):
                line(j, tile_at(at + w), lax.rem(lax.div(at, 2), 2) * 2 + w)

        def pairs(low, count, done):
            xb = [
                jnp.broadcast_to(xs[t // G, t % G : t % G + 1, :], (8, LANES))
                for t in range(m)
            ]

            @pl.loop(0, count // 2)
            def _(pair):
                at = low + pair * 2
                if j == 0:
                    for w in range(2):
                        tile_copy(tile_at(at + w)).wait()
                half = lax.rem(lax.div(at, 2), 2) * 2
                for w in range(2):
                    line(j, tile_at(jnp.maximum(at - 2, done) + w), 2 - half + w)
                for w in range(2):
                    slot = lax.rem(tile_at(at + w), slots)
                    for u in range(0, LANES, 8):
                        total = None
                        for t in range(m):
                            term = pool[slot, u : u + 8, t * LANES : (t + 1) * LANES] * xb[t]
                            total = term if total is None else total + term
                        acc[half + w, u : u + 8, :] = total

        if j == 0:
            def one(k):
                start = k * G
                pairs(start, G, start)
                finish(start + G - 2)
                p_targets(j, lax.div(tile_at(start), G))

                @pl.loop(start, jnp.minimum(start + G, spill))
                def _(at):
                    tile_copy(tile_at(slots + at)).start()

            middle = groups // 2 + 1
            pl.loop(0, middle)(one)
            late()
            pl.loop(middle, groups)(one)
            return

        ends = [k * ng for k in range(1, q + 1)]
        if ng > 1:
            ends += range(groups - ng + 1, groups)
        assert groups > 1
        cuts = sorted({0, *ends, min(groups, pl.cdiv(spill, G)), slots // G})
        sent_to = 0
        for low, high in zip(cuts, cuts[1:]):
            if high * G > slots:
                @pl.loop(max(low * G, slots), high * G)
                def _(at):
                    tile_copy(tile_at(at)).wait()

            pairs(low * G, (high - low) * G, sent_to * G)
            if high in ends:
                finish(jnp.int32(high * G - 2))
                if high == cuts[-2]:
                    late()
                first = groups - high if back else sent_to
                p_targets(j, jnp.int32(first), high - sent_to)
                sent_to = high
            if low * G < spill:
                @pl.loop(low * G, min(high * G, spill))
                def _(at):
                    tile_copy(tile_at(slots + at)).start()

    for w in range(4):
        acc[w] = jnp.zeros((LANES, LANES), jnp.float32)
    zero = jnp.zeros((1, 1), jnp.float32)
    arrived(av.at[pl.ds(0, 1)], av_sem.at[0])

    for j in range(K):
        if j == 0:
            x = load(av, 0)
        store(xs, [jnp.where(w > j + 1, a, 0.0) for w, a in zip(places(), x)])
        x_top_row = jnp.where(first_col, x[0][0:1, :], 0.0)
        sbuf[j, 0] = jnp.zeros((8, LANES), jnp.float32)
        sbuf[j, 1] = jnp.zeros((8, LANES), jnp.float32)
        sbuf[j, 0 if j else 1, K + 1 : K + 2, :] = x_top_row

        if j:
            for i in range(j):
                sbuf[j, 0, i : i + 1, :] = dots(load(vs, i), x)
            round_send(j, 0)
            if j + 1 == K:
                o_targets(vy.at[j - 1], ob.at[j - 1], j - 1)
            if j + 1 == K:
                o_targets(xs, ox, j)
        else:
            b = load(xs)
            sbuf[j, 1, K : K + 1, :] = dots(b, b)
            round_send(j, 1)
        def second_round():
            if j == 0:
                arrived(av.at[pl.ds(1, K)], av_sem.at[1])
                o_targets(av, oav, K)
                return
            got = round_get(j, 0)
            left = [lane_total(got[i : i + 1, :]) for i in range(j)]
            b, b_top = load(xs), got[K + 1 : K + 2, :]
            for k in range(j):
                total = zero
                for i in range(k + 1):
                    total = total + scalar(T_AT(i, k)) * left[i]
                keep(W_AT(k), total)
                b = less(b, total, load(vs, k))
                b_top = b_top - total * row_of(TOP_AT(k))
            keep(W_AT(K), b_top)
            b = [jnp.where(at > j + 1, a, 0.0) for at, a in zip(places(), b)]
            store(bs, b)
            for i in range(j):
                sbuf[j, 1, i : i + 1, :] = dots(load(vs, i), b)
            sbuf[j, 1, K : K + 1, :] = dots(b, b)
            round_send(j, 1)

        multiply(j, second_round)

        if j:
            w = [scalar(W_AT(i)) for i in range(j)]
            b, b_top = load(bs), row_of(W_AT(K))
            if j + 1 < K:
                o_targets(vy.at[j - 1], ob.at[j - 1], j - 1)
            p_sent(j - 1)
            r_sent(j - 1, 1)
            if j > 1:
                o_sent(ob.at[j - 2], j - 2)
                r_sent(j - 1, 0)
        else:
            w = []

            @pl.when(c == 0)
            def _():
                panel_sends(sent)

        got = round_get(j, 1)
        if j == 0:
            b_top = got[K + 1 : K + 2, :]
        v_top = [row_of(TOP_AT(i)) for i in range(j)]
        squares = lane_total(got[K : K + 1, :])
        pivot = pick(b_top, j + 1)
        length = jnp.sqrt(pivot * pivot + squares)
        beta = -jnp.where(pivot >= 0, 1.0, -1.0) * length
        tau = (beta - pivot) / beta
        div = pivot - beta
        cross = [lane_total(got[i : i + 1, :]) / div + pick(v_top[i], j + 1) for i in range(j)]
        new_top = jnp.where(lane1 > j + 1, b_top / div, 0.0) + jnp.where(lane1 == j + 1, 1.0, 0.0)
        keep(TOP_AT(j), new_top)
        for i in range(j):
            total = zero
            for k in range(i, j):
                total = total + scalar(T_AT(i, k)) * cross[k]
            keep(T_AT(i, j), -tau * total)
            keep(CROSS_AT(i, j), cross[i])
        keep(T_AT(j, j), tau)
        back = []
        for k in range(j + 2 if j else 0):
            total = zero
            for i in range(j):
                total = total + w[i] * pick(v_top[i], k)
            back.append(total)

        if j + 1 == K:
            break

        v = [a / div + jnp.where(at == j + 1, 1.0, 0.0) for at, a in zip(places(), b)]
        store(vs, v, j)
        store(vy, v, j, 1)
        fix = [jnp.zeros((G, LANES), jnp.float32)] * ng
        for i in range(j):
            fix = less(fix, w[i], load(ps, i))
        for k, value in enumerate(back):
            fix = less(fix, -value, load(av, k))
        y_fix = load(av, j + 1)
        for i in range(j):
            y_fix = less(y_fix, cross[i], load(ys, i))
        x = load(av, j + 1)
        for i in range(j):
            x = less(x, pick(v_top[i], j + 1), load(ys, i))
        entry = pick(new_top, j + 1)

        arrived(rbuf.at[j], p_recv.at[j])
        p = load(rbuf, j, 0)
        for n in range(1, C):
            p = [a + b_ for a, b_ in zip(p, load(rbuf, j, n))]
        p = [(a + e) / div for a, e in zip(p, fix)]
        y = [tau * (a + e) for a, e in zip(p, y_fix)]
        x = less(x, entry, y)
        store(vy, y, j, 0)
        store(ys, y, j)
        store(ps, [a + e for a, e in zip(p, load(av, j + 1))], j)

    scale = tau / div
    y_part, a_part = [], []
    for i in range(K - 1):
        total = w[i] / scalar(T_AT(i, i))
        for k in range(i + 1, K - 1):
            total = total + w[k] * scalar(CROSS_AT(i, k))
        y_part.append(-tau * (total / div + cross[i]))
    for k in range(K + 1):
        a_part.append(scale * back[k] + (tau if k == K else 0.0))
    for j in range(K - 1):
        arrived(ob.at[j], o_recv.at[j])
    arrived(ox, o_recv.at[K - 1])
    arrived(oav, o_recv.at[K])
    for g in range(groups):
        h, n = g // ng, g % ng
        at = index[ng + g]
        b = ox[h, n]
        rest = a_part[0] * oav[h, 0, n]
        for k in range(1, K + 1):
            rest = rest + a_part[k] * oav[h, k, n]
        for i in range(K - 1):
            y, v = ob[i, h, 0, n], ob[i, h, 1, n]
            o_ref[i, h, 0, n] = y
            o_ref[i, h, 1, n] = v
            b = b - w[i] * v
            rest = rest + y_part[i] * y
        v = jnp.where(at > K, b, 0.0) / div + jnp.where(at == K, 1.0, 0.0)
        o_ref[K - 1, h, 1, n] = v
        o_ref[K - 1, h, 0, n] = rest

    ti = lax.broadcasted_iota(jnp.int32, (K, K), 0)
    tj = lax.broadcasted_iota(jnp.int32, (K, K), 1)
    t_all = jnp.zeros((K, K), jnp.float32)
    for j in range(K):
        for i in range(j + 1):
            t_all = jnp.where(jnp.logical_and(ti == i, tj == j), scalar(T_AT(i, j)), t_all)
    t_ref[...] = t_all

    r_sent(K - 1, 0)
    r_sent(K - 1, 1)
    o_sent(ob.at[K - 2], K - 2)
    o_sent(ox, K - 1)
    o_sent(oav, K)
    arrived(lbuf.at[pl.ds(0, C - 1)], p_recv.at[K - 1])
    for g in range(groups):
        total = lbuf[0, g]
        for n in range(1, C):
            total = total + lbuf[n, g]
        h, n = g // ng, g % ng
        o_ref[K - 1, h, 0, n] = scale * total + o_ref[K - 1, h, 0, n]
    p_sent(K - 1)


def lay_out(o_ref, t_in, y_ref, v_ref, t_ref):
    _, q, _, ng, G, _ = o_ref.shape
    for h in range(q):
        for n in range(ng):
            for s in range(G):
                at = ((h * ng + n) * G + s) * LANES
                for j in range(K):
                    y_ref[j : j + 1, at : at + LANES] = o_ref[j, h, 0, n, s : s + 1, :]
                    v_ref[j : j + 1, at : at + LANES] = o_ref[j, h, 1, n, s : s + 1, :]
    t_ref[...] = t_in[...]


def solution(mesh):
    R, C = mesh.shape["row"], mesh.shape["col"]

    def on_device(matrix):
        rows, cols = matrix.shape
        q, m, G, ng, groups, slots = plan(R, C, rows, cols)
        f32 = lambda *shape: pltpu.VMEM(shape, jnp.float32)
        dma = lambda *shape: pltpu.SemaphoreType.DMA(shape)
        blocks, t_block = pl.pallas_call(
            functools.partial(kernel, R, C),
            out_shape=(
                jax.ShapeDtypeStruct((K, q, 2, ng, G, LANES), jnp.float32),
                jax.ShapeDtypeStruct((K, K), jnp.float32),
            ),
            in_specs=[pl.BlockSpec(memory_space=pl.ANY)],
            out_specs=(pl.BlockSpec(memory_space=pltpu.VMEM),) * 2,
            scratch_shapes=[
                f32(slots, LANES, cols),
                f32(4, LANES, LANES),
                f32(K + 1, groups, G, LANES),
                f32(K + 1, ng, G, LANES),
                f32(ng, G, LANES),
                f32(K, groups, G, LANES),
                f32(K - 1, C, ng, G, LANES),
                f32(C, groups, G, LANES),
                f32(K, 2, 8, LANES),
                f32(K, 2, C, 8, LANES),
                f32(K - 1, 2, ng, G, LANES),
                f32(K - 1, q, 2, ng, G, LANES),
                f32(q, K + 1, ng, G, LANES),
                f32(q, ng, G, LANES),
                f32(K - 1, ng, G, LANES),
                f32(K - 1, ng, G, LANES),
                f32(K - 1, ng, G, LANES),
                f32(ng, G, LANES),
                f32(2 * K * K + 2 * K + 1, LANES),
                pltpu.VMEM((ng + groups, G, LANES), jnp.int32),
                dma(slots),
                pltpu.SemaphoreType.DMA,
                dma(2, q, R),
                dma(2),
                dma(K),
                dma(K),
                dma(K, 2),
                dma(K, 2),
                dma(K + 1),
                dma(K + 1),
            ],
            compiler_params=pltpu.CompilerParams(
                collective_id=0, has_side_effects=True, vmem_limit_bytes=VMEM_BYTES,

            ),
        )(matrix)
        return pl.pallas_call(
            lay_out,
            out_shape=(
                jax.ShapeDtypeStruct((K, rows), jnp.float32),
                jax.ShapeDtypeStruct((K, rows), jnp.float32),
                jax.ShapeDtypeStruct((K, K), jnp.float32),
            ),
            in_specs=[pl.BlockSpec(memory_space=pltpu.VMEM)] * 2,
            out_specs=(pl.BlockSpec(memory_space=pltpu.VMEM),) * 3,
        )(blocks, t_block)

    return jax.shard_map(
        on_device,
        mesh=mesh,
        in_specs=(P("row", "col"),),
        out_specs=(P(None, "row"), P(None, "row"), P()),
        check_vma=False,
    )
```

```python
import functools

import jax
import jax.numpy as jnp
from jax import lax
from jax.experimental import pallas as pl
from jax.experimental.pallas import tpu as pltpu
from jax.sharding import PartitionSpec as P

K = 4
LANES = 128
MESH = pl.DeviceIdType.MESH
VMEM_BYTES = 67043328
SPARE_BYTES = 5 * 2**19


def plan(R, C, rows, cols):
    q = C // R
    m = cols // LANES
    G = 8 if m % 8 == 0 else m
    ng = m // G
    groups = q * ng
    room = (VMEM_BYTES - SPARE_BYTES) // (LANES * cols * 4)
    slots = min(groups * G, room) // 2 * 2
    assert 2 * slots >= groups * G and slots >= q and G % 2 == 0 and slots % 2 == 0
    return q, m, G, ng, groups, slots


def lane_total(row):
    return jnp.sum(row, axis=-1, keepdims=True)


def kernel(
    R, C, a_hbm, o_ref, t_ref,
    pool, acc, pan, av, xs, pbuf, rbuf, lbuf, sbuf, rnd, vy, ob, oav, ox, vs, ys, ps, bs, kept, index,
    pool_sem, pan_sem, pan_send, av_sem, p_send, p_recv, s_send, s_recv, o_send, o_recv,
):
    rows, cols = a_hbm.shape
    q, m, G, ng, groups, slots = plan(R, C, rows, cols)
    tiles = groups * G
    spill = tiles - slots
    r = lax.axis_index("row")
    c = lax.axis_index("col")

    def send(src, dst, send_sem, recv_sem, tr, tc):
        same = jnp.logical_and(tr == r, tc == c)

        @pl.when(jnp.logical_not(same))
        def _():
            pltpu.make_async_remote_copy(
                src, dst, send_sem, recv_sem, device_id=(tr, tc), device_id_type=MESH
            ).start()

        @pl.when(same)
        def _():
            pltpu.make_async_copy(src, dst, recv_sem).start()

    def sent(src, dst, send_sem, recv_sem, tr, tc):
        same = jnp.logical_and(tr == r, tc == c)

        @pl.when(jnp.logical_not(same))
        def _():
            pltpu.make_async_remote_copy(
                src, dst, send_sem, recv_sem, device_id=(tr, tc), device_id_type=MESH
            ).wait_send()

    def arrived(ref, sem):
        pltpu.make_async_copy(ref, ref, sem).wait()

    def panel_copy(t):
        return pltpu.make_async_copy(
            a_hbm.at[pl.ds(pl.multiple_of(t * LANES, LANES), LANES), pl.ds(0, LANES)],
            pool.at[
                slots - q + lax.div(t, m), :,
                pl.ds(pl.multiple_of(lax.rem(t, m) * LANES, LANES), LANES),
            ],
            pan_sem,
        )

    @pl.when(c == 0)
    def _():
        @pl.loop(0, q * m)
        def _(t):
            panel_copy(t).start()

    def tile_copy(t):
        slot = lax.rem(t, slots)
        row = pl.multiple_of(t * LANES, LANES)
        return pltpu.make_async_copy(
            a_hbm.at[pl.ds(row, LANES)], pool.at[slot], pool_sem.at[slot]
        )

    @pl.loop(0, slots - q)
    def _(t):
        tile_copy(t).start()

    barrier = pltpu.get_barrier_semaphore()
    me = r * C + c

    @pl.loop(1, R * C)
    def _(k):
        t = lax.rem(me + k, R * C)
        pl.semaphore_signal(
            barrier, inc=1, device_id=(lax.div(t, C), lax.rem(t, C)), device_id_type=MESH
        )

    def panel_sends(act):
        for part in range(2):
            for piece in range(q):
                for tr in range(R):
                    first, count = (0, 1) if part == 0 else (1, K)
                    act(
                        pan.at[pl.ds(first, count), pl.ds(piece * ng, ng)],
                        av.at[pl.ds(first, count)],
                        pan_send.at[part, piece, tr],
                        av_sem.at[part],
                        jnp.int32(tr),
                        r * q + piece,
                    )

    @pl.when(c == 0)
    def _():
        arrived(pool.at[pl.ds(slots - q, q)], pan_sem)

        @pl.loop(0, groups)
        def _(g):
            slot = slots - q + lax.div(g, ng)
            for s in range(G):
                at = pl.multiple_of((lax.rem(g, ng) * G + s) * LANES, LANES)
                turned = pool[slot, :, pl.ds(at, LANES)].T
                for k in range(K + 1):
                    pan[k, g, s : s + 1, :] = turned[k : k + 1, :]

    @pl.loop(slots - q, slots)
    def _(t):
        tile_copy(t).start()

    pl.semaphore_wait(barrier, R * C - 1)

    @pl.when(c == 0)
    def _():
        panel_sends(send)

    sub = lax.broadcasted_iota(jnp.int32, (G, LANES), 0)
    lane = lax.broadcasted_iota(jnp.int32, (G, LANES), 1)
    for n in range(ng):
        index[n] = c * cols + (n * G + sub) * LANES + lane
    for g in range(groups):
        index[ng + g] = r * rows + (g * G + sub) * LANES + lane
    lane1 = lax.broadcasted_iota(jnp.int32, (1, LANES), 1)
    first_col = (jnp.zeros((1, LANES), jnp.int32) + c) == 0

    def load(ref, *at):
        return [ref[(*at, n)] for n in range(ng)]

    def store(ref, value, *at):
        for n in range(ng):
            ref[(*at, n)] = value[n]

    def pick(row, k):
        return lane_total(jnp.where(lane1 == k, row, 0.0))

    def dots(one, two):
        total = one[0] * two[0]
        for n in range(1, ng):
            total = total + one[n] * two[n]
        return jnp.sum(total, axis=0, keepdims=True)

    def less(value, scale, other):
        return [a - scale * b for a, b in zip(value, other)]

    def round_copy(j, k, o):
        tc = lax.rem(c + o, C)
        return pltpu.make_async_remote_copy(
            sbuf.at[j, k], rnd.at[j, k, c], s_send.at[j, k], s_recv.at[j, k],
            device_id=(r, tc), device_id_type=MESH,
        )

    def round_send(j, k):
        rnd[j, k, c] = sbuf[j, k]

        @pl.loop(1, C)
        def _(o):
            round_copy(j, k, o).start()

    def round_get(j, k):
        arrived(rnd.at[j, k, pl.ds(0, C - 1)], s_recv.at[j, k])
        total = rnd[j, k, 0]
        for n in range(1, C):
            total = total + rnd[j, k, n]
        return total

    def places():
        return [index[n] for n in range(ng)]

    def keep(at, value):
        kept[at : at + 1, :] = jnp.broadcast_to(value, (1, LANES))

    def row_of(at):
        return kept[at : at + 1, :]

    def scalar(at):
        return kept[at : at + 1, 0:1]

    def T_AT(i, j):
        return i * K + j

    def CROSS_AT(i, j):
        return K * K + i * K + j

    def TOP_AT(i):
        return 2 * K * K + i

    def push(src, dst, send_sem, recv_sem, tr, tc):
        pltpu.make_async_remote_copy(
            src, dst, send_sem, recv_sem, device_id=(tr, tc), device_id_type=MESH
        ).start()

    def W_AT(i):
        return 2 * K * K + K + i

    def p_targets(j, g, count=1):
        block = pbuf.at[j, pl.ds(g, count)]
        if j + 1 == K:
            for o in range(1, C):
                push(
                    block, lbuf.at[c, pl.ds(g, count)], p_send.at[j], p_recv.at[j], r,
                    lax.rem(c + o, C),
                )
            for n in range(count):
                lbuf[c, g + n] = pbuf[j, g + n]
            return
        piece, part = lax.div(g, ng), lax.rem(g, ng)
        there, tc = rbuf.at[j, c, pl.ds(part, count)], r * q + piece
        for o in range(1, R):
            push(block, there, p_send.at[j], p_recv.at[j], lax.rem(r + o, R), tc)
        send(block, there, p_send.at[j], p_recv.at[j], r, tc)

    def p_sent(j):
        if j + 1 == K:
            arrived(lbuf.at[pl.ds(0, C - 1)], p_send.at[j])
            return
        own = lax.div(c, q) == r

        @pl.when(own)
        def _():
            arrived(rbuf.at[j, pl.ds(0, C - 1)], p_send.at[j])

        @pl.when(jnp.logical_not(own))
        def _():
            arrived(rbuf.at[j], p_send.at[j])

    def o_targets(src, dst, k):
        for u in range(q):
            send(
                src, dst.at[lax.rem(c, q)], o_send.at[k], o_recv.at[k], lax.div(c, q), r + R * u
            )

    def o_sent(dst, k):
        own = jnp.logical_and(lax.div(c, q) == r, lax.rem(c, R) == r)

        @pl.when(own)
        def _():
            arrived(dst.at[pl.ds(0, q - 1)], o_send.at[k])

        @pl.when(jnp.logical_not(own))
        def _():
            arrived(dst, o_send.at[k])

    def r_sent(j, k):
        arrived(rnd.at[j, k, pl.ds(0, C - 1)], s_send.at[j, k])

    def line(j, tile, slot):
        pbuf[j, lax.div(tile, G), pl.ds(lax.rem(tile, G), 1), :] = jnp.sum(
            acc[slot].T, axis=0, keepdims=True
        )

    def multiply(j, late):
        back = j % 2 == 1

        def tile_at(at):
            return tiles - 1 - at if back else at

        def finish(at):
            for w in range(2):
                line(j, tile_at(at + w), lax.rem(lax.div(at, 2), 2) * 2 + w)

        def pairs(low, count, done):
            xb = [
                jnp.broadcast_to(xs[t // G, t % G : t % G + 1, :], (8, LANES))
                for t in range(m)
            ]

            @pl.loop(0, count // 2)
            def _(pair):
                at = low + pair * 2
                if j == 0:
                    for w in range(2):
                        tile_copy(tile_at(at + w)).wait()
                half = lax.rem(lax.div(at, 2), 2) * 2
                for w in range(2):
                    line(j, tile_at(jnp.maximum(at - 2, done) + w), 2 - half + w)
                for w in range(2):
                    slot = lax.rem(tile_at(at + w), slots)
                    for u in range(0, LANES, 8):
                        total = None
                        for t in range(m):
                            term = pool[slot, u : u + 8, t * LANES : (t + 1) * LANES] * xb[t]
                            total = term if total is None else total + term
                        acc[half + w, u : u + 8, :] = total

        if j == 0:
            def one(k):
                start = k * G
                pairs(start, G, start)
                finish(start + G - 2)
                p_targets(j, lax.div(tile_at(start), G))

                @pl.loop(start, jnp.minimum(start + G, spill))
                def _(at):
                    tile_copy(tile_at(slots + at)).start()

            middle = groups // 2 + 1
            pl.loop(0, middle)(one)
            late()
            pl.loop(middle, groups)(one)
            return

        ends = [k * ng for k in range(1, q + 1)]
        if ng > 1:
            ends += range(groups - ng + 1, groups)
        assert groups > 1
        cuts = sorted({0, *ends, min(groups, pl.cdiv(spill, G)), slots // G})
        sent_to = 0
        for low, high in zip(cuts, cuts[1:]):
            if high * G > slots:
                @pl.loop(max(low * G, slots), high * G)
                def _(at):
                    tile_copy(tile_at(at)).wait()

            pairs(low * G, (high - low) * G, sent_to * G)
            if low == 0 and j + 1 == K:
                o_targets(xs, ox, j)
                o_targets(vy.at[j - 1], ob.at[j - 1], j - 1)
            if high in ends:
                finish(jnp.int32(high * G - 2))
                if high == cuts[-2]:
                    late()
                first = groups - high if back else sent_to
                p_targets(j, jnp.int32(first), high - sent_to)
                sent_to = high
            if low * G < spill:
                @pl.loop(low * G, min(high * G, spill))
                def _(at):
                    tile_copy(tile_at(slots + at)).start()

    for w in range(4):
        acc[w] = jnp.zeros((LANES, LANES), jnp.float32)
    zero = jnp.zeros((1, 1), jnp.float32)
    arrived(av.at[pl.ds(0, 1)], av_sem.at[0])

    for j in range(K):
        if j == 0:
            x = load(av, 0)
        store(xs, [jnp.where(w > j + 1, a, 0.0) for w, a in zip(places(), x)])
        x_top_row = jnp.where(first_col, x[0][0:1, :], 0.0)
        sbuf[j, 0] = jnp.zeros((8, LANES), jnp.float32)
        sbuf[j, 1] = jnp.zeros((8, LANES), jnp.float32)
        sbuf[j, 0 if j else 1, K + 1 : K + 2, :] = x_top_row

        if j:
            for i in range(j):
                sbuf[j, 0, i : i + 1, :] = dots(load(vs, i), x)
            round_send(j, 0)
        else:
            b = load(xs)
            sbuf[j, 1, K : K + 1, :] = dots(b, b)
            round_send(j, 1)
        def second_round():
            if j == 0:
                arrived(av.at[pl.ds(1, K)], av_sem.at[1])
                o_targets(av, oav, K)
                return
            got = round_get(j, 0)
            left = [lane_total(got[i : i + 1, :]) for i in range(j)]
            b, b_top = load(xs), got[K + 1 : K + 2, :]
            for k in range(j):
                total = zero
                for i in range(k + 1):
                    total = total + scalar(T_AT(i, k)) * left[i]
                keep(W_AT(k), total)
                b = less(b, total, load(vs, k))
                b_top = b_top - total * row_of(TOP_AT(k))
            keep(W_AT(K), b_top)
            b = [jnp.where(at > j + 1, a, 0.0) for at, a in zip(places(), b)]
            store(bs, b)
            for i in range(j):
                sbuf[j, 1, i : i + 1, :] = dots(load(vs, i), b)
            sbuf[j, 1, K : K + 1, :] = dots(b, b)
            round_send(j, 1)

        multiply(j, second_round)

        if j:
            w = [scalar(W_AT(i)) for i in range(j)]
            b, b_top = load(bs), row_of(W_AT(K))
            if j + 1 < K:
                o_targets(vy.at[j - 1], ob.at[j - 1], j - 1)
            p_sent(j - 1)
            r_sent(j - 1, 1)
            if j > 1:
                o_sent(ob.at[j - 2], j - 2)
                r_sent(j - 1, 0)
        else:
            w = []

            @pl.when(c == 0)
            def _():
                panel_sends(sent)

        got = round_get(j, 1)
        if j == 0:
            b_top = got[K + 1 : K + 2, :]
        v_top = [row_of(TOP_AT(i)) for i in range(j)]
        squares = lane_total(got[K : K + 1, :])
        pivot = pick(b_top, j + 1)
        length = jnp.sqrt(pivot * pivot + squares)
        beta = -jnp.where(pivot >= 0, 1.0, -1.0) * length
        tau = (beta - pivot) / beta
        div = pivot - beta
        cross = [lane_total(got[i : i + 1, :]) / div + pick(v_top[i], j + 1) for i in range(j)]
        new_top = jnp.where(lane1 > j + 1, b_top / div, 0.0) + jnp.where(lane1 == j + 1, 1.0, 0.0)
        keep(TOP_AT(j), new_top)
        for i in range(j):
            total = zero
            for k in range(i, j):
                total = total + scalar(T_AT(i, k)) * cross[k]
            keep(T_AT(i, j), -tau * total)
            keep(CROSS_AT(i, j), cross[i])
        keep(T_AT(j, j), tau)
        back = []
        for k in range(j + 2 if j else 0):
            total = zero
            for i in range(j):
                total = total + w[i] * pick(v_top[i], k)
            back.append(total)

        if j + 1 == K:
            break

        v = [a / div + jnp.where(at == j + 1, 1.0, 0.0) for at, a in zip(places(), b)]
        store(vs, v, j)
        store(vy, v, j, 1)
        fix = [jnp.zeros((G, LANES), jnp.float32)] * ng
        for i in range(j):
            fix = less(fix, w[i], load(ps, i))
        for k, value in enumerate(back):
            fix = less(fix, -value, load(av, k))
        y_fix = load(av, j + 1)
        for i in range(j):
            y_fix = less(y_fix, cross[i], load(ys, i))
        x = load(av, j + 1)
        for i in range(j):
            x = less(x, pick(v_top[i], j + 1), load(ys, i))
        entry = pick(new_top, j + 1)

        arrived(rbuf.at[j], p_recv.at[j])
        p = load(rbuf, j, 0)
        for n in range(1, C):
            p = [a + b_ for a, b_ in zip(p, load(rbuf, j, n))]
        p = [(a + e) / div for a, e in zip(p, fix)]
        y = [tau * (a + e) for a, e in zip(p, y_fix)]
        x = less(x, entry, y)
        store(vy, y, j, 0)
        store(ys, y, j)
        store(ps, [a + e for a, e in zip(p, load(av, j + 1))], j)

    scale = tau / div
    y_part, a_part = [], []
    for i in range(K - 1):
        total = w[i] / scalar(T_AT(i, i))
        for k in range(i + 1, K - 1):
            total = total + w[k] * scalar(CROSS_AT(i, k))
        y_part.append(-tau * (total / div + cross[i]))
    for k in range(K + 1):
        a_part.append(scale * back[k] + (tau if k == K else 0.0))
    for j in range(K - 1):
        arrived(ob.at[j], o_recv.at[j])
    arrived(ox, o_recv.at[K - 1])
    arrived(oav, o_recv.at[K])
    for g in range(groups):
        h, n = g // ng, g % ng
        at = index[ng + g]
        b = ox[h, n]
        rest = a_part[0] * oav[h, 0, n]
        for k in range(1, K + 1):
            rest = rest + a_part[k] * oav[h, k, n]
        for i in range(K - 1):
            y, v = ob[i, h, 0, n], ob[i, h, 1, n]
            o_ref[i, h, 0, n] = y
            o_ref[i, h, 1, n] = v
            b = b - w[i] * v
            rest = rest + y_part[i] * y
        v = jnp.where(at > K, b, 0.0) / div + jnp.where(at == K, 1.0, 0.0)
        o_ref[K - 1, h, 1, n] = v
        o_ref[K - 1, h, 0, n] = rest

    ti = lax.broadcasted_iota(jnp.int32, (K, K), 0)
    tj = lax.broadcasted_iota(jnp.int32, (K, K), 1)
    t_all = jnp.zeros((K, K), jnp.float32)
    for j in range(K):
        for i in range(j + 1):
            t_all = jnp.where(jnp.logical_and(ti == i, tj == j), scalar(T_AT(i, j)), t_all)
    t_ref[...] = t_all

    r_sent(K - 1, 0)
    r_sent(K - 1, 1)
    o_sent(ob.at[K - 2], K - 2)
    o_sent(ox, K - 1)
    o_sent(oav, K)
    arrived(lbuf.at[pl.ds(0, C - 1)], p_recv.at[K - 1])
    for g in range(groups):
        total = lbuf[0, g]
        for n in range(1, C):
            total = total + lbuf[n, g]
        h, n = g // ng, g % ng
        o_ref[K - 1, h, 0, n] = scale * total + o_ref[K - 1, h, 0, n]
    p_sent(K - 1)


def lay_out(o_ref, t_in, y_ref, v_ref, t_ref):
    _, q, _, ng, G, _ = o_ref.shape
    for h in range(q):
        for n in range(ng):
            for s in range(G):
                at = ((h * ng + n) * G + s) * LANES
                for j in range(K):
                    y_ref[j : j + 1, at : at + LANES] = o_ref[j, h, 0, n, s : s + 1, :]
                    v_ref[j : j + 1, at : at + LANES] = o_ref[j, h, 1, n, s : s + 1, :]
    t_ref[...] = t_in[...]


def solution(mesh):
    R, C = mesh.shape["row"], mesh.shape["col"]

    def on_device(matrix):
        rows, cols = matrix.shape
        q, m, G, ng, groups, slots = plan(R, C, rows, cols)
        f32 = lambda *shape: pltpu.VMEM(shape, jnp.float32)
        dma = lambda *shape: pltpu.SemaphoreType.DMA(shape)
        blocks, t_block = pl.pallas_call(
            functools.partial(kernel, R, C),
            out_shape=(
                jax.ShapeDtypeStruct((K, q, 2, ng, G, LANES), jnp.float32),
                jax.ShapeDtypeStruct((K, K), jnp.float32),
            ),
            in_specs=[pl.BlockSpec(memory_space=pl.ANY)],
            out_specs=(pl.BlockSpec(memory_space=pltpu.VMEM),) * 2,
            scratch_shapes=[
                f32(slots, LANES, cols),
                f32(4, LANES, LANES),
                f32(K + 1, groups, G, LANES),
                f32(K + 1, ng, G, LANES),
                f32(ng, G, LANES),
                f32(K, groups, G, LANES),
                f32(K - 1, C, ng, G, LANES),
                f32(C, groups, G, LANES),
                f32(K, 2, 8, LANES),
                f32(K, 2, C, 8, LANES),
                f32(K - 1, 2, ng, G, LANES),
                f32(K - 1, q, 2, ng, G, LANES),
                f32(q, K + 1, ng, G, LANES),
                f32(q, ng, G, LANES),
                f32(K - 1, ng, G, LANES),
                f32(K - 1, ng, G, LANES),
                f32(K - 1, ng, G, LANES),
                f32(ng, G, LANES),
                f32(2 * K * K + 2 * K + 1, LANES),
                pltpu.VMEM((ng + groups, G, LANES), jnp.int32),
                dma(slots),
                pltpu.SemaphoreType.DMA,
                dma(2, q, R),
                dma(2),
                dma(K),
                dma(K),
                dma(K, 2),
                dma(K, 2),
                dma(K + 1),
                dma(K + 1),
            ],
            compiler_params=pltpu.CompilerParams(
                collective_id=0, has_side_effects=True, vmem_limit_bytes=VMEM_BYTES,

            ),
        )(matrix)
        return pl.pallas_call(
            lay_out,
            out_shape=(
                jax.ShapeDtypeStruct((K, rows), jnp.float32),
                jax.ShapeDtypeStruct((K, rows), jnp.float32),
                jax.ShapeDtypeStruct((K, K), jnp.float32),
            ),
            in_specs=[pl.BlockSpec(memory_space=pltpu.VMEM)] * 2,
            out_specs=(pl.BlockSpec(memory_space=pltpu.VMEM),) * 3,
        )(blocks, t_block)

    return jax.shard_map(
        on_device,
        mesh=mesh,
        in_specs=(P("row", "col"),),
        out_specs=(P(None, "row"), P(None, "row"), P()),
        check_vma=False,
    )
```
